32 devices in a mesh: seq: 8 (over y, x, core), rep: 4 (over z).
Axes of the slice: x: 2, y: 2, z: 4, core: 2. Of those that a mesh axis runs over, the one named last changes fastest.
Arguments:
- hidden_in: bfloat16 [4, 4096, 1024], P('rep', 'seq'), may hold values from -6 to 6
- segments: int32 [4, 4096], P('rep', 'seq'), may hold values from 0 to 3, never falling along the last dimension, each value on 1 to 2048 neighbouring positions
- w_in: bfloat16 [1024, 4384], P(('seq', 'rep')), may hold values from -0.1875 to 0.1875
- w_out: bfloat16 [2048, 1024], P(('seq', 'rep')), may hold values from -0.125 to 0.125
- norm_gain: float32 [1024], replicated, may hold values from 0.5 to 1.5
- conv_w: float32 [4, 2304], replicated, may hold values from -3 to 3
- conv_b: float32 [2304], replicated, may hold values from -0.5 to 0.5
- dt_bias: float32 [32], replicated, may hold values from -7 to -2.5
- a_log: float32 [32], replicated, may hold values from 0 to 2.77
- d_skip: float32 [32], replicated, may hold values from 0.5 to 1.5
- gate_gain: float32 [2048], replicated, may hold values from 0.5 to 1.5
- cotangent: bfloat16 [4, 4096, 1024], P('rep', 'seq'), may hold values from -6 to 6
Outputs:
- block_out: bfloat16 [4, 4096, 1024], P('rep', 'seq')
- d_hidden: float32 [4, 4096, 1024], P('rep', 'seq')
- d_w_in: float32 [1024, 4384], P(('seq', 'rep'))
- d_w_out: float32 [2048, 1024], P(('seq', 'rep'))
- d_norm_gain: float32 [1024], replicated
- d_conv_w: float32 [4, 2304], replicated
- d_conv_b: float32 [2304], replicated
- d_dt_bias: float32 [32], replicated
- d_a_log: float32 [32], replicated
- d_d_skip: float32 [32], replicated
- d_gate_gain: float32 [2048], replicated
The draws below stay inside these ranges and needn't reach their ends.
Inputs may be any that keep to these rules, and one draw needn't show every extreme that they name: `segments`: along each sequence the numbers start at 0 and rise by one at each document start; a document holds 1 to 2048 tokens, one holds exactly 2048.
All inputs are finite; a program needn't handle non-finite values.
Results may differ from the reference program's by a relative error of at most 0.011.
Values may be sent and summed in bfloat16 or wider, within the bound.
No kernel may reach another device: no remote copies, remote signals or barrier semaphores. Data moves between devices by JAX's collectives and lax.ppermute only.
A program may use at most 192 MiB of HBM per device.

```python
import math
import jax
import jax.numpy as jnp
import numpy as np
from jax import lax

D = 1024
HEADS = 32
CONV = 4
GROUP = 256
DOC_MOST = 2048
INNER = 2048
XBC = 2304
PROJ = 4384
SEQS = 4
LENGTH = 4096
DOCS = 4


def spiked(array, key, source, target, blocks, factor):
    def block_of(position):
        return (jnp.arange(array.shape[position]) // (array.shape[position] // blocks)).reshape((-1,) + (1,) * (array.ndim - 1 - position))

    one_side = jax.random.permutation(key, blocks)[block_of(target)]
    second = (block_of(target) + blocks // 2) % blocks
    return jnp.where((block_of(source) == one_side) | (block_of(source) == second), factor * array, array)


def block_levels(rng, shape, pieces, smallest, top_value):
    def one(dim, blocks):
        draws = jax.random.uniform(jax.random.fold_in(jax.random.fold_in(rng, 6), dim), (blocks,), jnp.float32, smallest / len(pieces), top_value / len(pieces))
        return jnp.repeat(jnp.exp(draws), shape[dim] // blocks).reshape((-1,) + (1,) * (len(shape) - dim - 1))

    loudness = one(*pieces[0])
    for cut in pieces[1:]:
        loudness = loudness * one(*cut)
    return loudness


def profile(count, total, most, skew):
    portions = [(1 << 20) // math.isqrt(standing ** skew) + 1 for standing in range(2, count + 1)]
    surplus, given = total - most - (count - 1), [1] * (count - 1)
    while surplus > 0:
        candidates = [i for i in range(count - 1) if given[i] < most]
        pool, left = sum([portions[i] for i in candidates]), surplus
        for i in candidates:
            addition = min(most - given[i], max(1, left * portions[i] // pool), surplus)
            given[i] = given[i] + addition
            surplus = surplus - addition
    return np.array([most] + given)


def ragged_sizes(key, number_of, total, limit, slope):
    if number_of == 2:
        one = jax.random.randint(key, (), max(1, total - limit), min(limit, total - 1) + 1)
        return jnp.stack([one, total - one])
    tallies = jnp.asarray(profile(number_of, total, limit, slope), jnp.int32)
    pairs = (number_of - 1) // 2
    donor, sink = tallies[1:1 + 2 * pairs:2], tallies[2:2 + 2 * pairs:2]
    slack = jnp.minimum(donor - 1, limit - sink)
    shifted = jax.random.randint(jax.random.fold_in(key, 1), (pairs,), 0, 1 << 20) % (slack + 1)
    tallies = tallies.at[1:1 + 2 * pairs:2].set(donor - shifted).at[2:2 + 2 * pairs:2].set(sink + shifted)
    return tallies[jax.random.permutation(jax.random.fold_in(key, 2), number_of)]


def noise(stream_key, dims, scale, limit, shards=(), kind=jnp.bfloat16):
    values = jax.random.normal(stream_key, dims, jnp.float32) * scale
    if len(shards) > 0:
        values = block_levels(stream_key, dims, shards, -0.22, 0.18) * values
    return jnp.clip(values, min=-limit, max=limit).astype(kind)


def bell_draw_with(own_key, extent, scale, limit, shards, heavy, held_as=jnp.bfloat16):
    entries = scale * jax.random.normal(own_key, extent, jnp.float32)
    if shards:
        entries = entries * block_levels(own_key, extent, shards, -0.22, 0.18)
    return jnp.clip(spiked(entries, jax.random.fold_in(own_key, 3), *heavy), -limit, limit).astype(held_as)


def setup_inputs(seed: int = 0) -> dict:
    seeds = jax.random.split(jax.random.key(seed), 13)
    return {
        "hidden_in": bell_draw_with(seeds[0], (SEQS, LENGTH, D), 1.0, 6.0, ((0, 4), (1, 8)), (1, 2, 8, 2.0)),
        "segments": jax.vmap(lambda own: jnp.searchsorted(jnp.cumsum(ragged_sizes(own, DOCS, LENGTH, DOC_MOST, 1)), jnp.arange(LENGTH), side="right"))(jax.random.split(seeds[1], SEQS)).reshape((SEQS, LENGTH)).astype(jnp.int32),
        "w_in": noise(seeds[2], (D, PROJ), D ** -0.5, 0.1875, ((0, 32),)),
        "w_out": noise(seeds[3], (INNER, D), INNER ** -0.5, 0.125, ((0, 32),)),
        "norm_gain": jnp.clip(1.0 + 0.1 * jax.random.normal(seeds[4], (D,), jnp.float32), 0.5, 1.5),
        "conv_w": noise(seeds[5], (CONV, XBC), CONV ** -0.5, 3.0, (), jnp.float32),
        "conv_b": jnp.clip(jax.random.uniform(seeds[6], (XBC,), jnp.float32, -0.5, 0.5), -0.5, 0.5),
        "dt_bias": jnp.clip(jax.random.uniform(seeds[7], (HEADS,), jnp.float32, -7.0, -2.5), -7.0, -2.5),
        "a_log": jnp.clip(jax.random.uniform(seeds[8], (HEADS,), jnp.float32, 0.0, 2.77), 0.0, 2.77),
        "d_skip": jnp.clip(jax.random.uniform(seeds[9], (HEADS,), jnp.float32, 0.5, 1.5), 0.5, 1.5),
        "gate_gain": jnp.clip(1.0 + 0.1 * jax.random.normal(seeds[10], (INNER,), jnp.float32), 0.5, 1.5),
        "cotangent": noise(seeds[11], (SEQS, LENGTH, D), 1.0, 6.0, ((0, 4), (1, 8))),
    }


NORM_EPS = 1e-05

def product(spec, left, right):
    return jnp.einsum(spec, left.astype(jnp.float32), right.astype(jnp.float32))

def expand(values, head_dim):
    return jnp.repeat(values, head_dim)[:, None]

def group_terms(x_blk, b_blk, c_blk, step_blk, log_blk, seg_blk, seg_prev):
    length = x_blk.shape[0]
    cum_log = jnp.cumsum(log_blk, axis=0)
    positions = jnp.arange(length)
    lower_mask = positions[:, None] >= positions[None, :]
    same_doc = (seg_blk[:, None] == seg_blk[None, :]) & lower_mask
    cum_heads = cum_log.T
    spread = cum_heads[:, :, None] - cum_heads[:, None, :]
    decays = jnp.where(same_doc[None], jnp.exp(jnp.where(same_doc[None], spread, 0.0)), 0.0)
    inner_cb = product('tn,sn->ts', c_blk, b_blk)
    weights = inner_cb[None] * decays * step_blk.T[:, None, :]
    to_end = jnp.where((seg_blk == seg_blk[-1])[:, None], jnp.exp(cum_log[-1][None, :] - cum_log), 0.0)
    from_start = jnp.where((seg_blk == seg_prev)[:, None], jnp.exp(cum_log), 0.0)
    block_decay = jnp.where(seg_blk[-1] == seg_prev, jnp.exp(cum_log[-1]), 0.0)
    return (decays, inner_cb, weights, to_end, from_start, block_decay)

def group_forward(x_blk, b_blk, c_blk, step_blk, log_blk, seg_blk, seg_prev, head_count):
    length, width_all = x_blk.shape
    head_dim = width_all // head_count
    decays, inner_cb, weights, to_end, from_start, block_decay = group_terms(x_blk, b_blk, c_blk, step_blk, log_blk, seg_blk, seg_prev)
    x_heads = x_blk.reshape(length, head_count, head_dim)
    mix_b16 = weights.astype(jnp.bfloat16)
    y_inner = product('hts,shp->thp', mix_b16, x_heads).reshape(length, width_all)
    state_weight = to_end * step_blk
    x_weighted = (x_heads.astype(jnp.float32) * state_weight[:, :, None]).reshape(length, width_all).astype(jnp.bfloat16)
    block_state = product('se,sn->en', x_weighted, b_blk)
    return (y_inner, block_state, block_decay, from_start)

def state_grad(grad_blk, from_start, c_blk, head_count):
    length, width_all = grad_blk.shape
    head_dim = width_all // head_count
    grad_start = (grad_blk.reshape(length, head_count, head_dim) * from_start[:, :, None]).reshape(length, width_all).astype(jnp.bfloat16)
    return product('te,tn->en', grad_start, c_blk)

def group_backward(x_blk, b_blk, c_blk, step_blk, log_blk, seg_blk, seg_prev, grad_blk, h_blk, d_next, head_count):
    length, width_all = x_blk.shape
    head_dim = width_all // head_count
    decays, inner_cb, weights, to_end, from_start, block_decay = group_terms(x_blk, b_blk, c_blk, step_blk, log_blk, seg_blk, seg_prev)
    x_heads = x_blk.reshape(length, head_count, head_dim)
    mix_b16 = weights.astype(jnp.bfloat16)
    grad_b16 = grad_blk.astype(jnp.bfloat16).reshape(length, head_count, head_dim)
    d_x = product('hts,thp->shp', mix_b16, grad_b16)
    d_mix = product('thp,shp->hts', grad_b16, x_heads)
    d_masked = d_mix * decays
    d_inner = lax.optimization_barrier(jnp.sum(d_masked * step_blk.T[:, None, :], axis=0)).astype(jnp.bfloat16)
    d_c = product('ts,sn->tn', d_inner, b_blk)
    d_b = product('ts,tn->sn', d_inner, c_blk)
    d_step = lax.optimization_barrier(jnp.sum(d_masked * inner_cb[None], axis=1)).T
    d_cross = d_mix * weights
    d_cum = (lax.optimization_barrier(jnp.sum(d_cross, axis=2)) - lax.optimization_barrier(jnp.sum(d_cross, axis=1))).T
    h_b16 = h_blk.astype(jnp.bfloat16)
    y_cross = product('tn,en->te', c_blk, h_b16).reshape(length, head_count, head_dim)
    grad_heads = grad_blk.reshape(length, head_count, head_dim)
    d_cum = d_cum + lax.optimization_barrier(jnp.sum(grad_heads * y_cross, axis=2)) * from_start
    grad_start = (grad_heads * from_start[:, :, None]).reshape(length, width_all).astype(jnp.bfloat16)
    d_c = d_c + product('te,en->tn', grad_start, h_b16)
    d_next_b16 = d_next.astype(jnp.bfloat16)
    state_weight = to_end * step_blk
    x_weighted = (x_heads.astype(jnp.float32) * state_weight[:, :, None]).reshape(length, width_all).astype(jnp.bfloat16)
    d_b = d_b + product('se,en->sn', x_weighted, d_next_b16)
    d_weighted = product('sn,en->se', b_blk, d_next_b16).reshape(length, head_count, head_dim)
    d_x = d_x + d_weighted * state_weight[:, :, None]
    d_wt = lax.optimization_barrier(jnp.sum(d_weighted * x_heads.astype(jnp.float32), axis=2))
    d_step = d_step + d_wt * to_end
    d_to_end = d_wt * state_weight
    d_block = lax.optimization_barrier(jnp.sum((d_next * h_blk).reshape(head_count, head_dim * h_blk.shape[1]), axis=1))
    end_add = lax.optimization_barrier(jnp.sum(d_to_end, axis=0)) + d_block * block_decay
    last_row = (jnp.arange(length) == length - 1)[:, None]
    d_cum = d_cum - d_to_end + jnp.where(last_row, end_add[None, :], 0.0)
    d_log = jnp.flip(jnp.cumsum(jnp.flip(d_cum, 0), axis=0), 0)
    return (d_x.reshape(length, width_all), d_b, d_c, d_step, d_log)

def conv_forward(rows_pad, seg_pad, segment, conv_w, conv_b):
    length = segment.shape[0]
    tap_count = conv_w.shape[0]
    running = jnp.zeros((length, conv_w.shape[1]), jnp.float32) + conv_b[None, :]
    for tap_index in range(tap_count):
        keep_mask = (seg_pad[tap_index:tap_index + length] == segment)[:, None]
        running = running + jnp.where(keep_mask, conv_w[tap_index][None, :] * rows_pad[tap_index:tap_index + length], 0.0)
    return running

def conv_backward(d_pre, rows_pad, seg_pad, next_rows, next_ids, segment, conv_w):
    length = segment.shape[0]
    tap_count = conv_w.shape[0]
    d_pad = jnp.concatenate([d_pre, next_rows], axis=0)
    seg_after = jnp.concatenate([segment, next_ids], axis=0)
    d_conv_in = jnp.zeros_like(d_pre)
    tap_rows = []
    for tap_index in range(tap_count):
        keep_in = (seg_pad[tap_index:tap_index + length] == segment)[:, None]
        tap_rows.append(lax.optimization_barrier(jnp.sum(jnp.where(keep_in, d_pre * rows_pad[tap_index:tap_index + length], 0.0), axis=0)))
        shift_by = tap_count - 1 - tap_index
        keep_out = (seg_after[shift_by:shift_by + length] == segment)[:, None]
        d_conv_in = d_conv_in + jnp.where(keep_out, conv_w[tap_index][None, :] * d_pad[shift_by:shift_by + length], 0.0)
    return (d_conv_in, jnp.stack(tap_rows), lax.optimization_barrier(jnp.sum(d_pre, axis=0)))

def sequence_pass(hidden_seq, segment, grad_seq, w_in, w_out, norm_gain, conv_w, conv_b, dt_bias, a_log, d_skip, gate_gain):
    head_count = dt_bias.shape[0]
    inner_width = gate_gain.shape[0]
    head_dim = inner_width // head_count
    xbc_width = conv_w.shape[1]
    state_dim = (xbc_width - inner_width) // 2
    tap_count = conv_w.shape[0]
    length = hidden_seq.shape[0]
    blocks = length // GROUP
    hidden32 = hidden_seq.astype(jnp.float32)
    norm_scale = lax.rsqrt(lax.optimization_barrier(jnp.mean(hidden32 * hidden32, axis=-1, keepdims=True)) + NORM_EPS)
    normed = (hidden32 * norm_scale * norm_gain).astype(jnp.bfloat16)
    projected = jnp.dot(normed, w_in, preferred_element_type=jnp.float32).astype(jnp.bfloat16)
    gate_raw = projected[:, :inner_width].astype(jnp.float32)
    conv_in = projected[:, inner_width:inner_width + xbc_width]
    step_raw = projected[:, inner_width + xbc_width:].astype(jnp.float32)
    rows_pad = jnp.concatenate([jnp.zeros((tap_count - 1, xbc_width), jnp.float32), conv_in.astype(jnp.float32)], axis=0)
    seg_pad = jnp.concatenate([jnp.full((tap_count - 1,), -1, jnp.int32), segment], axis=0)
    conv_pre = conv_forward(rows_pad, seg_pad, segment, conv_w, conv_b)
    conv_out = jax.nn.silu(conv_pre).astype(jnp.bfloat16)
    x_part = conv_out[:, :inner_width]
    b_part = conv_out[:, inner_width:inner_width + state_dim]
    c_part = conv_out[:, inner_width + state_dim:]
    step_pre = step_raw + dt_bias
    step_size = jax.nn.softplus(step_pre)
    decay_rate = -jnp.exp(a_log)
    log_decay = step_size * decay_rate
    prev_token = jnp.concatenate([segment[:1], segment[:-1]], axis=0)
    group_prev = prev_token.reshape(blocks, GROUP)[:, 0]
    x_c = x_part.reshape(blocks, GROUP, inner_width)
    b_c = b_part.reshape(blocks, GROUP, state_dim)
    c_c = c_part.reshape(blocks, GROUP, state_dim)
    step_c = step_size.reshape(blocks, GROUP, head_count)
    log_c = log_decay.reshape(blocks, GROUP, head_count)
    seg_c = segment.reshape(blocks, GROUP)

    def forward_step(h_now, inputs):
        x_blk, b_blk, c_blk, step_blk, log_blk, seg_blk, seg_prev = inputs
        y_inner, block_state, block_decay, from_start = group_forward(x_blk, b_blk, c_blk, step_blk, log_blk, seg_blk, seg_prev, head_count)
        y_cross = product('tn,en->te', c_blk, h_now.astype(jnp.bfloat16)).reshape(GROUP, head_count, head_dim)
        y_blk = y_inner + (from_start[:, :, None] * y_cross).reshape(GROUP, inner_width)
        h_next = expand(block_decay, head_dim) * h_now + block_state
        return (h_next, (y_blk, h_now, from_start, block_decay))
    _, (ssd_blocks, h_blocks, from_starts, block_decays) = lax.scan(forward_step, jnp.zeros((inner_width, state_dim), jnp.float32), (x_c, b_c, c_c, step_c, log_c, seg_c, group_prev))
    x32 = x_part.astype(jnp.float32)
    ssd_out = ssd_blocks.reshape(length, inner_width) + (x32.reshape(length, head_count, head_dim) * d_skip[None, :, None]).reshape(length, inner_width)
    gate_sig = jax.nn.sigmoid(gate_raw)
    gate_act = gate_raw * gate_sig
    gated = ssd_out * gate_act
    gate_scale = lax.rsqrt(lax.optimization_barrier(jnp.mean(gated * gated, axis=-1, keepdims=True)) + NORM_EPS)
    gate_normed = (gated * gate_scale * gate_gain).astype(jnp.bfloat16)
    mixed = jnp.dot(gate_normed, w_out, preferred_element_type=jnp.float32)
    block_out = (hidden32 + mixed).astype(jnp.bfloat16)
    grad32 = grad_seq.astype(jnp.float32)
    d_w_out = jnp.dot(gate_normed.T, grad_seq, preferred_element_type=jnp.float32)
    d_gate_normed = jnp.dot(grad_seq, w_out.T, preferred_element_type=jnp.float32)
    gate_term = d_gate_normed * gate_gain
    d_gate_gain = lax.optimization_barrier(jnp.sum(d_gate_normed * gated * gate_scale, axis=0))
    d_gated = gate_scale * gate_term - gated * gate_scale ** 3 * lax.optimization_barrier(jnp.mean(gate_term * gated, axis=-1, keepdims=True))
    d_ssd = d_gated * gate_act
    d_gate_raw = d_gated * ssd_out * gate_sig * (1.0 + gate_raw * (1.0 - gate_sig))
    d_d_skip = lax.optimization_barrier(jnp.sum((d_ssd * x32).reshape(length, head_count, head_dim), axis=(0, 2)))
    d_x_skip = (d_ssd.reshape(length, head_count, head_dim) * d_skip[None, :, None]).reshape(length, inner_width)
    d_y_c = d_ssd.reshape(blocks, GROUP, inner_width)

    def backward_step(d_now, inputs):
        x_blk, b_blk, c_blk, step_blk, log_blk, seg_blk, seg_prev, grad_blk, h_blk, from_start, block_decay = inputs
        parts = group_backward(x_blk, b_blk, c_blk, step_blk, log_blk, seg_blk, seg_prev, grad_blk, h_blk, d_now, head_count)
        d_prev = state_grad(grad_blk, from_start, c_blk, head_count) + expand(block_decay, head_dim) * d_now
        return (d_prev, parts)
    _, (d_x_c, d_b_c, d_c_c, d_step_c, d_log_c) = lax.scan(backward_step, jnp.zeros((inner_width, state_dim), jnp.float32), (x_c, b_c, c_c, step_c, log_c, seg_c, group_prev, d_y_c, h_blocks, from_starts, block_decays), reverse=True)
    d_x = d_x_c.reshape(length, inner_width) + d_x_skip
    d_conv_out = jnp.concatenate([d_x, d_b_c.reshape(length, state_dim), d_c_c.reshape(length, state_dim)], axis=1)
    conv_sig = jax.nn.sigmoid(conv_pre)
    d_pre = d_conv_out * conv_sig * (1.0 + conv_pre * (1.0 - conv_sig))
    next_rows = jnp.zeros((tap_count - 1, xbc_width), jnp.float32)
    next_ids = jnp.full((tap_count - 1,), -1, jnp.int32)
    d_conv_in, d_conv_w, d_conv_b = conv_backward(d_pre, rows_pad, seg_pad, next_rows, next_ids, segment, conv_w)
    d_log = d_log_c.reshape(length, head_count)
    d_step = d_step_c.reshape(length, head_count) + d_log * decay_rate
    d_a_log = lax.optimization_barrier(jnp.sum(d_log * step_size, axis=0)) * decay_rate
    d_step_raw = d_step * jax.nn.sigmoid(step_pre)
    d_dt_bias = lax.optimization_barrier(jnp.sum(d_step_raw, axis=0))
    d_projected = jnp.concatenate([d_gate_raw, d_conv_in, d_step_raw], axis=1).astype(jnp.bfloat16)
    d_w_in = jnp.dot(normed.T, d_projected, preferred_element_type=jnp.float32)
    d_normed = jnp.dot(d_projected, w_in.T, preferred_element_type=jnp.float32)
    norm_term = d_normed * norm_gain
    d_norm_gain = lax.optimization_barrier(jnp.sum(d_normed * hidden32 * norm_scale, axis=0))
    d_hidden = grad32 + norm_scale * norm_term - hidden32 * norm_scale ** 3 * lax.optimization_barrier(jnp.mean(norm_term * hidden32, axis=-1, keepdims=True))
    grads = (d_w_in, d_w_out, d_norm_gain, d_conv_w, d_conv_b, d_dt_bias, d_a_log, d_d_skip, d_gate_gain)
    return (block_out, d_hidden, grads)

def reference(hidden_in, segments, w_in, w_out, norm_gain, conv_w, conv_b, dt_bias, a_log, d_skip, gate_gain, cotangent):

    def one_sequence(carry, inputs):
        hidden_seq, segment, grad_seq = inputs
        block_out, d_hidden, grads = sequence_pass(hidden_seq, segment, grad_seq, w_in, w_out, norm_gain, conv_w, conv_b, dt_bias, a_log, d_skip, gate_gain)
        summed = tuple((running + term for running, term in zip(carry, grads)))
        return (summed, (block_out, d_hidden))
    zeros_init = tuple((jnp.zeros(param.shape, jnp.float32) for param in (w_in, w_out, norm_gain, conv_w, conv_b, dt_bias, a_log, d_skip, gate_gain)))
    totals, (block_outs, d_hiddens) = lax.scan(one_sequence, zeros_init, (hidden_in, segments, cotangent))
    return (block_outs, d_hiddens, totals[0], totals[1], totals[2], totals[3], totals[4], totals[5], totals[6], totals[7], totals[8])
```

```python
import jax
import jax.numpy as jnp
from jax import lax
from jax.sharding import PartitionSpec as P

GROUP = 256


NORM_EPS = 1e-05


def shifted(value, axis, steps):
    count = lax.axis_size(axis)
    initial, last = (max(0, -steps), min(count, count - steps))
    return lax.ppermute(value, axis, [(source, source + steps) for source in range(initial, last)])


DOC_MOST = 2048


def log2(count):
    return count.bit_length() - 1


def swap(value, axis, bit):
    count = lax.axis_size(axis)
    return lax.ppermute(value, axis, [(i, i ^ (1 << bit)) for i in range(count)])


def bit_orders():
    high = list(range(1, log2(lax.axis_size("seq"))))
    cut = len(high) // 2
    return (high[cut:] + high[:cut], high[:cut] + high[cut:])


def to_relative(value):
    count = lax.axis_size("seq")
    unit = value.shape[1] // count
    own = lax.axis_index("seq")
    return jnp.concatenate(
        [
            lax.dynamic_slice_in_dim(value, (own ^ r) * unit, unit, axis=1)
            for r in range(count)
        ],
        axis=1,
    )


def gather_rows(local, high_order):
    rep = lax.axis_index("rep")
    value = local
    for bit in range(log2(lax.axis_size("rep"))):
        other = swap(value, "rep", bit)
        value = jnp.where(
            ((rep >> bit) & 1) == 1,
            jnp.concatenate([other, value], axis=0),
            jnp.concatenate([value, other], axis=0),
        )
    pieces = [(0, value)]
    for bit in list(high_order) + [0]:
        message = jnp.concatenate([piece for _, piece in pieces], axis=0)
        arrived = swap(message, "seq", bit)
        rows = value.shape[0]
        pieces = pieces + [
            (key | (1 << bit), arrived[i * rows : (i + 1) * rows])
            for i, (key, _) in enumerate(pieces)
        ]
    return jnp.concatenate([piece for _, piece in sorted(pieces, key=lambda p: p[0])], axis=0)


def scatter_rows(full, high_order):
    rep = lax.axis_index("rep")
    count = lax.axis_size("seq")
    unit = full.shape[0] // count
    pieces = [(r, full[r * unit : (r + 1) * unit]) for r in range(count)]
    for bit in [0] + list(reversed(high_order)):
        keep = [(key, piece) for key, piece in pieces if not (key >> bit) & 1]
        send = jnp.concatenate([piece for key, piece in pieces if (key >> bit) & 1], axis=0)
        arrived = swap(send, "seq", bit)
        total = jnp.concatenate([piece for _, piece in keep], axis=0) + arrived
        pieces = [(key, total[i * unit : (i + 1) * unit]) for i, (key, _) in enumerate(keep)]
    value = pieces[0][1]
    for bit in reversed(range(log2(lax.axis_size("rep")))):
        half = value.shape[0] // 2
        mine = (rep >> bit) & 1
        send = lax.dynamic_slice_in_dim(value, (1 - mine) * half, half, axis=0)
        keep = lax.dynamic_slice_in_dim(value, mine * half, half, axis=0)
        value = keep + swap(send, "rep", bit)
    return value


def reduce_all(value):
    for axis in ("seq", "rep"):
        for bit in range(log2(lax.axis_size(axis))):
            value = value + swap(value, axis, bit)
    return value


def relay(state, decay, length, forward):
    count = lax.axis_size("seq")
    window = -(-(DOC_MOST - 1) // length)
    chips = count // 2
    hops = min(-(-window // 2), chips - 1)
    lead = 1 if forward else 0
    step = 1 if forward else -1
    is_lead = (lax.axis_index("seq") & 1) == lead

    def send(value, pairs):
        return lax.ppermute(value, "seq", pairs)

    to_lead = [(2 * c + 1 - lead, 2 * c + lead) for c in range(chips)]
    to_other = [(2 * c + lead, 2 * c + 1 - lead) for c in range(chips)]
    other_state, other_decay = send((state.astype(jnp.bfloat16), decay), to_lead)
    other_state = other_state.astype(jnp.float32)
    chip_state = (state + decay * other_state).astype(jnp.bfloat16)
    chip_decay = decay * other_decay
    entering = jnp.zeros_like(state)
    arrived = []
    for hop in range(1, hops + 1):
        pairs = [
            (2 * c + lead, 2 * (c + step * hop) + lead)
            for c in range(chips)
            if 0 <= c + step * hop < chips
        ]
        arrived.append(send((chip_state, chip_decay), pairs))
    for chip_part, decay_part in reversed(arrived):
        entering = chip_part.astype(jnp.float32) + decay_part * entering
    handed = send(entering.astype(jnp.bfloat16), to_other).astype(jnp.float32)
    return jnp.where(is_lead, other_state + other_decay * entering, handed)


def product(spec, left, right):
    return jnp.einsum(spec, left, right, preferred_element_type=jnp.float32)


def expand(values, head_dim):
    return jnp.repeat(values, head_dim)[:, None]


def group_terms(x_blk, b_blk, c_blk, step_blk, log_blk, seg_blk, seg_prev):
    length = x_blk.shape[0]
    cum_log = jnp.cumsum(log_blk, axis=0)
    positions = jnp.arange(length)
    lower_mask = positions[:, None] >= positions[None, :]
    same_doc = (seg_blk[:, None] == seg_blk[None, :]) & lower_mask
    cum_heads = cum_log.T
    spread = cum_heads[:, :, None] - cum_heads[:, None, :]
    decays = jnp.where(same_doc[None], jnp.exp(jnp.where(same_doc[None], spread, 0.0)), 0.0)
    inner_cb = product("tn,sn->ts", c_blk, b_blk)
    weights = inner_cb[None] * decays * step_blk.T[:, None, :]
    to_end = jnp.where(
        (seg_blk == seg_blk[-1])[:, None], jnp.exp(cum_log[-1][None, :] - cum_log), 0.0
    )
    from_start = jnp.where((seg_blk == seg_prev)[:, None], jnp.exp(cum_log), 0.0)
    block_decay = jnp.where(seg_blk[-1] == seg_prev, jnp.exp(cum_log[-1]), 0.0)
    return (decays, inner_cb, weights, to_end, from_start, block_decay)


def group_forward(x_blk, b_blk, c_blk, step_blk, log_blk, seg_blk, seg_prev, head_count):
    length, width_all = x_blk.shape
    head_dim = width_all // head_count
    decays, inner_cb, weights, to_end, from_start, block_decay = group_terms(
        x_blk, b_blk, c_blk, step_blk, log_blk, seg_blk, seg_prev
    )
    x_heads = x_blk.reshape(length, head_count, head_dim)
    mix_b16 = weights.astype(jnp.bfloat16)
    y_inner = product("hts,shp->thp", mix_b16, x_heads).reshape(length, width_all)
    state_weight = to_end * step_blk
    x_weighted = (
        (x_heads.astype(jnp.float32) * state_weight[:, :, None])
        .reshape(length, width_all)
        .astype(jnp.bfloat16)
    )
    block_state = product("se,sn->en", x_weighted, b_blk)
    return (y_inner, block_state, block_decay, from_start)


def state_grad(grad_blk, from_start, c_blk, head_count):
    length, width_all = grad_blk.shape
    head_dim = width_all // head_count
    grad_start = (
        (grad_blk.reshape(length, head_count, head_dim) * from_start[:, :, None])
        .reshape(length, width_all)
        .astype(jnp.bfloat16)
    )
    return product("te,tn->en", grad_start, c_blk)


def group_backward(
    x_blk, b_blk, c_blk, step_blk, log_blk, seg_blk, seg_prev, grad_blk, h_blk, d_next, head_count
):
    length, width_all = x_blk.shape
    head_dim = width_all // head_count
    decays, inner_cb, weights, to_end, from_start, block_decay = group_terms(
        x_blk, b_blk, c_blk, step_blk, log_blk, seg_blk, seg_prev
    )
    x_heads = x_blk.reshape(length, head_count, head_dim)
    mix_b16 = weights.astype(jnp.bfloat16)
    grad_b16 = grad_blk.astype(jnp.bfloat16).reshape(length, head_count, head_dim)
    d_x = product("hts,thp->shp", mix_b16, grad_b16)
    d_mix = product("thp,shp->hts", grad_b16, x_heads)
    d_masked = d_mix * decays
    d_inner = jnp.sum(d_masked * step_blk.T[:, None, :], axis=0).astype(jnp.bfloat16)
    d_c = product("ts,sn->tn", d_inner, b_blk)
    d_b = product("ts,tn->sn", d_inner, c_blk)
    d_step = jnp.sum(d_masked * inner_cb[None], axis=1).T
    d_cross = d_mix * weights
    d_cum = (jnp.sum(d_cross, axis=2) - jnp.sum(d_cross, axis=1)).T
    h_b16 = h_blk.astype(jnp.bfloat16)
    y_cross = product("tn,en->te", c_blk, h_b16).reshape(length, head_count, head_dim)
    grad_heads = grad_blk.reshape(length, head_count, head_dim)
    d_cum = d_cum + jnp.sum(grad_heads * y_cross, axis=2) * from_start
    grad_start = (
        (grad_heads * from_start[:, :, None]).reshape(length, width_all).astype(jnp.bfloat16)
    )
    d_c = d_c + product("te,en->tn", grad_start, h_b16)
    d_next_b16 = d_next.astype(jnp.bfloat16)
    state_weight = to_end * step_blk
    x_weighted = (
        (x_heads.astype(jnp.float32) * state_weight[:, :, None])
        .reshape(length, width_all)
        .astype(jnp.bfloat16)
    )
    d_b = d_b + product("se,en->sn", x_weighted, d_next_b16)
    d_weighted = product("sn,en->se", b_blk, d_next_b16).reshape(length, head_count, head_dim)
    d_x = d_x + d_weighted * state_weight[:, :, None]
    d_wt = jnp.sum(d_weighted * x_heads.astype(jnp.float32), axis=2)
    d_step = d_step + d_wt * to_end
    d_to_end = d_wt * state_weight
    d_block = jnp.sum((d_next * h_blk).reshape(head_count, head_dim * h_blk.shape[1]), axis=1)
    end_add = jnp.sum(d_to_end, axis=0) + d_block * block_decay
    last_row = (jnp.arange(length) == length - 1)[:, None]
    d_cum = d_cum - d_to_end + jnp.where(last_row, end_add[None, :], 0.0)
    d_log = jnp.flip(jnp.cumsum(jnp.flip(d_cum, 0), axis=0), 0)
    return (d_x.reshape(length, width_all), d_b, d_c, d_step, d_log)


def conv_forward(rows_pad, seg_pad, segment, conv_w, conv_b):
    length = segment.shape[0]
    tap_count = conv_w.shape[0]
    running = jnp.zeros((length, conv_w.shape[1]), jnp.float32) + conv_b[None, :]
    for tap_index in range(tap_count):
        keep_mask = (seg_pad[tap_index : tap_index + length] == segment)[:, None]
        running = running + jnp.where(
            keep_mask, conv_w[tap_index][None, :] * rows_pad[tap_index : tap_index + length], 0.0
        )
    return running


def conv_backward(d_pre, rows_pad, seg_pad, next_rows, next_ids, segment, conv_w):
    length = segment.shape[0]
    tap_count = conv_w.shape[0]
    d_pad = jnp.concatenate([d_pre, next_rows], axis=0)
    seg_after = jnp.concatenate([segment, next_ids], axis=0)
    d_conv_in = jnp.zeros_like(d_pre)
    tap_rows = []
    for tap_index in range(tap_count):
        keep_in = (seg_pad[tap_index : tap_index + length] == segment)[:, None]
        tap_rows.append(
            jnp.sum(
                jnp.where(keep_in, d_pre * rows_pad[tap_index : tap_index + length], 0.0), axis=0
            )
        )
        shift_by = tap_count - 1 - tap_index
        keep_out = (seg_after[shift_by : shift_by + length] == segment)[:, None]
        d_conv_in = d_conv_in + jnp.where(
            keep_out, conv_w[tap_index][None, :] * d_pad[shift_by : shift_by + length], 0.0
        )
    return (d_conv_in, jnp.stack(tap_rows), jnp.sum(d_pre, axis=0))


def fold_rows(left, portion):
    return jnp.dot(left, portion, preferred_element_type=jnp.float32)


def spread_rows(left, portion):
    return jnp.einsum("tk,rk->tr", left, portion, preferred_element_type=jnp.float32)


def row_term(left, right):
    return jnp.einsum("tr,tk->rk", left, right, preferred_element_type=jnp.float32)


def per_device(
    hidden_in,
    segments,
    w_in,
    w_out,
    norm_gain,
    conv_w,
    conv_b,
    dt_bias,
    a_log,
    d_skip,
    gate_gain,
    cotangent,
):
    head_count = dt_bias.shape[0]
    inner_width = gate_gain.shape[0]
    head_dim = inner_width // head_count
    xbc_width = conv_w.shape[1]
    state_dim = (xbc_width - inner_width) // 2
    tap_count = conv_w.shape[0]
    tokens = hidden_in[0]
    segment = segments[0].astype(jnp.float32)
    grad_seq = cotangent[0]
    length = tokens.shape[0]
    blocks = length // GROUP
    hidden32 = tokens.astype(jnp.float32)
    norm_scale = lax.rsqrt(jnp.mean(hidden32 * hidden32, axis=-1, keepdims=True) + NORM_EPS)
    normed = (hidden32 * norm_scale * norm_gain).astype(jnp.bfloat16)
    normed_rel = to_relative(normed)
    first, second = bit_orders()
    cut = inner_width + xbc_width // 2
    w_a = gather_rows(w_in[:, inner_width:cut], first)
    w_b = gather_rows(w_in[:, cut:], second)
    w_g = gather_rows(w_in[:, :inner_width], first)
    wo = gather_rows(w_out, second)
    conv_in = jnp.concatenate(
        [fold_rows(normed_rel, w_a), fold_rows(normed_rel, w_b)], axis=1
    ).astype(jnp.bfloat16)
    step_raw = conv_in[:, xbc_width:].astype(jnp.float32)
    conv_in = conv_in[:, :xbc_width]
    gate_raw = fold_rows(normed_rel, w_g).astype(jnp.bfloat16).astype(jnp.float32)
    edge_rows = conv_in[length - tap_count + 1 :].astype(jnp.float32)
    prev_rows, prev_ids = shifted((edge_rows, segment[length - tap_count + 1 :]), "seq", 1)
    rows_pad = jnp.concatenate([prev_rows, conv_in.astype(jnp.float32)], axis=0)
    seg_pad = jnp.concatenate([prev_ids, segment], axis=0)
    conv_pre = conv_forward(rows_pad, seg_pad, segment, conv_w, conv_b)
    conv_out = jax.nn.silu(conv_pre).astype(jnp.bfloat16)
    x_part = conv_out[:, :inner_width]
    b_part = conv_out[:, inner_width : inner_width + state_dim]
    c_part = conv_out[:, inner_width + state_dim :]
    step_pre = step_raw + dt_bias
    step_size = jax.nn.softplus(step_pre)
    decay_rate = -jnp.exp(a_log)
    log_decay = step_size * decay_rate
    prev_token = jnp.concatenate([prev_ids[-1:], segment[:-1]], axis=0)
    group_prev = prev_token.reshape(blocks, GROUP)[:, 0]
    x_c = x_part.reshape(blocks, GROUP, inner_width)
    b_c = b_part.reshape(blocks, GROUP, state_dim)
    c_c = c_part.reshape(blocks, GROUP, state_dim)
    step_c = step_size.reshape(blocks, GROUP, head_count)
    log_c = log_decay.reshape(blocks, GROUP, head_count)
    seg_c = segment.reshape(blocks, GROUP)
    y_inner, block_states, block_decays, from_starts = lax.map(
        lambda inputs: group_forward(*inputs, head_count),
        (x_c, b_c, c_c, step_c, log_c, seg_c, group_prev),
    )

    def compose(carry, inputs):
        decay_now, state_now = inputs
        return ((carry[0] * decay_now, expand(decay_now, head_dim) * carry[1] + state_now), None)

    ones_heads = jnp.ones((head_count,), jnp.float32)
    zero_state = jnp.zeros((inner_width, state_dim), jnp.float32)
    (dev_decay, dev_state), _ = lax.scan(
        compose, (ones_heads, zero_state), (block_decays, block_states)
    )

    h_start = relay(dev_state, expand(dev_decay, head_dim), length, True)

    def advance(h_now, inputs):
        decay_now, state_now = inputs
        return (expand(decay_now, head_dim) * h_now + state_now, h_now)

    _, h_blocks = lax.scan(advance, h_start, (block_decays, block_states))
    y_cross = product("ctn,cen->cte", c_c, h_blocks.astype(jnp.bfloat16)).reshape(
        blocks, GROUP, head_count, head_dim
    )
    ssd_blocks = y_inner + (from_starts[:, :, :, None] * y_cross).reshape(
        blocks, GROUP, inner_width
    )
    x32 = x_part.astype(jnp.float32)
    ssd_out = ssd_blocks.reshape(length, inner_width) + (
        x32.reshape(length, head_count, head_dim) * d_skip[None, :, None]
    ).reshape(length, inner_width)
    gate_sig = jax.nn.sigmoid(gate_raw)
    gate_act = gate_raw * gate_sig
    gated = ssd_out * gate_act
    gate_scale = lax.rsqrt(jnp.mean(gated * gated, axis=-1, keepdims=True) + NORM_EPS)
    gate_normed = (gated * gate_scale * gate_gain).astype(jnp.bfloat16)
    gate_rel = to_relative(gate_normed)
    mixed = fold_rows(gate_rel, wo)
    block_out = (hidden32 + mixed).astype(jnp.bfloat16)
    grad32 = grad_seq.astype(jnp.float32)
    d_w_out = scatter_rows(row_term(gate_rel, grad_seq).astype(jnp.bfloat16), second).astype(
        jnp.float32
    )
    d_gate_normed = to_relative(spread_rows(grad_seq, wo))
    gate_term = d_gate_normed * gate_gain
    d_gate_gain = jnp.sum(d_gate_normed * gated * gate_scale, axis=0)
    d_gated = gate_scale * gate_term - gated * gate_scale**3 * jnp.mean(
        gate_term * gated, axis=-1, keepdims=True
    )
    d_ssd = d_gated * gate_act
    d_gate_raw = d_gated * ssd_out * gate_sig * (1.0 + gate_raw * (1.0 - gate_sig))
    d_d_skip = jnp.sum((d_ssd * x32).reshape(length, head_count, head_dim), axis=(0, 2))
    d_x_skip = (d_ssd.reshape(length, head_count, head_dim) * d_skip[None, :, None]).reshape(
        length, inner_width
    )
    d_y_c = d_ssd.reshape(blocks, GROUP, inner_width)
    local_grads = lax.map(lambda inputs: state_grad(*inputs, head_count), (d_y_c, from_starts, c_c))

    def gather_back(running, inputs):
        decay_now, grad_now = inputs
        return (grad_now + expand(decay_now, head_dim) * running, None)

    dev_grad, _ = lax.scan(gather_back, zero_state, (block_decays, local_grads), reverse=True)

    grad_next = relay(dev_grad, expand(dev_decay, head_dim), length, False)

    def retreat(d_now, inputs):
        decay_now, grad_now = inputs
        return (grad_now + expand(decay_now, head_dim) * d_now, d_now)

    _, d_nexts = lax.scan(retreat, grad_next, (block_decays, local_grads), reverse=True)
    d_x_c, d_b_c, d_c_c, d_step_c, d_log_c = lax.map(
        lambda inputs: group_backward(*inputs, head_count),
        (x_c, b_c, c_c, step_c, log_c, seg_c, group_prev, d_y_c, h_blocks, d_nexts),
    )
    d_x = d_x_c.reshape(length, inner_width) + d_x_skip
    d_conv_out = jnp.concatenate(
        [d_x, d_b_c.reshape(length, state_dim), d_c_c.reshape(length, state_dim)], axis=1
    )
    conv_sig = jax.nn.sigmoid(conv_pre)
    d_pre = d_conv_out * conv_sig * (1.0 + conv_pre * (1.0 - conv_sig))
    next_rows, next_ids = shifted((d_pre[: tap_count - 1], segment[: tap_count - 1]), "seq", -1)
    d_conv_in, d_conv_w, d_conv_b = conv_backward(
        d_pre, rows_pad, seg_pad, next_rows, next_ids, segment, conv_w
    )
    d_log = d_log_c.reshape(length, head_count)
    d_step = d_step_c.reshape(length, head_count) + d_log * decay_rate
    d_a_log = jnp.sum(d_log * step_size, axis=0) * decay_rate
    d_step_raw = d_step * jax.nn.sigmoid(step_pre)
    d_dt_bias = jnp.sum(d_step_raw, axis=0)
    d_gate_b16 = d_gate_raw.astype(jnp.bfloat16)
    d_rest = jnp.concatenate([d_conv_in, d_step_raw], axis=1).astype(jnp.bfloat16)
    part = xbc_width // 2
    d_w_g = scatter_rows(row_term(normed_rel, d_gate_b16).astype(jnp.bfloat16), first)
    d_w_a = scatter_rows(row_term(normed_rel, d_rest[:, :part]).astype(jnp.bfloat16), first)
    d_w_b = scatter_rows(row_term(normed_rel, d_rest[:, part:]).astype(jnp.bfloat16), second)
    d_w_in = jnp.concatenate([d_w_g, d_w_a, d_w_b], axis=1).astype(jnp.float32)
    d_normed = to_relative(
        spread_rows(d_gate_b16, w_g)
        + spread_rows(d_rest[:, :part], w_a)
        + spread_rows(d_rest[:, part:], w_b)
    )
    norm_term = d_normed * norm_gain
    d_norm_gain = jnp.sum(d_normed * hidden32 * norm_scale, axis=0)
    d_hidden = (
        grad32
        + norm_scale * norm_term
        - hidden32 * norm_scale**3 * jnp.mean(norm_term * hidden32, axis=-1, keepdims=True)
    )
    small = (d_norm_gain, d_conv_w, d_conv_b, d_dt_bias, d_a_log, d_d_skip, d_gate_gain)
    flat = reduce_all(jnp.concatenate([part.reshape(-1) for part in small]))
    summed, at = [], 0
    for part in small:
        summed.append(flat[at : at + part.size].reshape(part.shape))
        at += part.size
    return (
        block_out[None],
        d_hidden[None],
        d_w_in,
        d_w_out,
        summed[0],
        summed[1],
        summed[2],
        summed[3],
        summed[4],
        summed[5],
        summed[6],
    )


def solution(mesh):
    in_specs = (
        P("rep", "seq", None),
        P("rep", "seq"),
        P(("seq", "rep"), None),
        P(("seq", "rep"), None),
        P(),
        P(),
        P(),
        P(),
        P(),
        P(),
        P(),
        P("rep", "seq", None),
    )
    out_specs = (
        P("rep", "seq", None),
        P("rep", "seq", None),
        P(("seq", "rep"), None),
        P(("seq", "rep"), None),
        P(),
        P(),
        P(),
        P(),
        P(),
        P(),
        P(),
    )
    return jax.shard_map(
        per_device, mesh=mesh, in_specs=in_specs, out_specs=out_specs, check_vma=False
    )
```
